32 devices in a mesh: rows: 16 (over z, y, x), rep: 2 (over core).
Axes of the slice: x: 2, y: 2, z: 4, core: 2. Of those that a mesh axis runs over, the one named last changes fastest.
Arguments:
- features: bfloat16 [4096, 256], P(('rows', 'rep')), may hold values from -6 to 6
- weight: bfloat16 [256, 256], replicated, may hold values from -0.375 to 0.375
- adj_tiles: bfloat16 [32, 2, 10, 128, 128], P('rows', 'rep'), may hold values from -0.25 to 0.25
- tile_cols: int32 [32, 2, 10], P('rows', 'rep'), may hold values from 0 to 15
- tile_counts: int32 [32, 2], P('rows', 'rep'), may hold values from 1 to 10, as said below
- out_grad: bfloat16 [4096, 256], P(('rows', 'rep')), may hold values from -6 to 6
- train_mask: int32 [4096], P(('rows', 'rep')), may hold values 0 or 1
Outputs:
- activations: bfloat16 [4096, 256], P(('rows', 'rep'))
- feat_grad: bfloat16 [4096, 256], P(('rows', 'rep'))
- weight_step: float32 [256, 256], replicated
The draws below stay inside these ranges and needn't reach their ends.
Inputs may be any that keep to these rules, and one draw needn't show every extreme that they name: Only the first tile_counts slots of a tile row are used; some tile row has all 10 slots live. `tile_cols`: columns may repeat within a tile row.
All inputs are finite; a program needn't handle non-finite values. No bound on the sum of `train_mask` on one device may be relied on, other than what follows from the above.
Results may differ from the reference program's by a relative error of at most 0.0062.
Values may be sent and summed in bfloat16 or wider, within the bound.
A program may use at most 64 MiB of HBM per device.

```python
import jax
import jax.numpy as jnp
from jax import lax

D = 256
TILE = 128
K = 10
NODE_DEV = 128
TR_ALL = 32
TC = 16
NODES = 4096
N_ROWS = 16
N_REP = 2


def draw_tile_counts(key, part):
    first_key, second_key = jax.random.split(jax.random.fold_in(key, 17))
    base_counts = jax.random.randint(first_key, (TR_ALL * N_REP,), 1, K + 1)
    full_spot = jax.random.randint(second_key, (), 0, TR_ALL * N_REP)
    positions = jnp.arange(TR_ALL * N_REP, dtype=jnp.int32)
    counts_flat = jnp.where(positions == full_spot, K, base_counts)
    return counts_flat.reshape(TR_ALL, N_REP).astype(jnp.int32)


def plant(values, own_key, least, top_value):
    index_at = [jax.random.randint(jax.random.fold_in(own_key, axis), (), 0, length) for axis, length in enumerate(values.shape)]
    widest = values.shape.index(max(values.shape))
    neighbour = index_at[:widest] + [(index_at[widest] + 1) % values.shape[widest]] + index_at[widest + 1:]
    return values.at[tuple(index_at)].set(least).at[tuple(neighbour)].set(top_value)


def level_of(key, extent, cuts, low, top_value):
    def one(position, shards_of):
        steps = jax.random.uniform(jax.random.fold_in(jax.random.fold_in(key, 6), position), (shards_of,), jnp.float32, low / len(cuts), top_value / len(cuts))
        return jnp.repeat(jnp.exp(steps), extent[position] // shards_of).reshape((-1,) + (1,) * (len(extent) - position - 1))

    gain = one(*cuts[0])
    for cut in cuts[1:]:
        gain = gain * one(*cut)
    return gain


def noise(own_key, dims, scale, most, pieces=(), kind=jnp.bfloat16):
    entries = scale * jax.random.normal(own_key, dims, jnp.float32)
    if pieces:
        entries = entries * level_of(own_key, dims, pieces, -0.22, 0.18)
    return jnp.clip(entries, -most, most).astype(kind)


def setup_inputs(seed: int = 0) -> dict:
    streams_of = jax.random.split(jax.random.key(seed), 8)
    return {
        "features": noise(streams_of[0], (NODES, D), 1.0, 6.0, ((0, 32),)),
        "weight": noise(streams_of[1], (D, D), D ** -0.5, 0.375),
        "adj_tiles": noise(streams_of[2], (TR_ALL, N_REP, K, TILE, TILE), (TILE * K // 2) ** -0.5, 0.25, ((0, 16), (1, 2))),
        "tile_cols": plant(jax.random.randint(streams_of[3], (TR_ALL, N_REP, K), 0, TC), jax.random.fold_in(streams_of[3], 1), 0, TC - 1).astype(jnp.int32),
        "tile_counts": draw_tile_counts(jax.random.fold_in(streams_of[7], 71), 0),
        "out_grad": noise(streams_of[5], (NODES, D), 1.0, 6.0, ((0, 32),)),
        "train_mask": plant((jax.random.randint(streams_of[6], (NODES,), 0, 4) < 1).astype(jnp.int32), jax.random.fold_in(streams_of[6], 1), 0, 1),
    }


def reference(features, weight, adj_tiles, tile_cols, tile_counts, out_grad, train_mask):
    group_feat = features.reshape(N_ROWS, N_REP, NODE_DEV, D).transpose(1, 0, 2, 3).reshape(N_REP, TC, TILE, D)
    live_mask = (jnp.arange(K, dtype=jnp.int32)[None, None, :] < tile_counts[:, :, None]).astype(jnp.float32)
    group_index = jnp.arange(N_REP, dtype=jnp.int32)[:, None]
    tile_index = jnp.arange(TR_ALL, dtype=jnp.int32)

    def forward_row(tile_row):
        adj_block = adj_tiles[tile_row].astype(jnp.float32) * live_mask[tile_row][:, :, None, None]
        picked = group_feat[group_index, tile_cols[tile_row]].astype(jnp.float32)
        return jnp.einsum('jkab,jkbd->ad', adj_block, picked)
    aggregated = lax.map(forward_row, tile_index).reshape(NODES, D).astype(jnp.bfloat16)
    pre_act = jnp.dot(aggregated, weight, preferred_element_type=jnp.float32)
    activations = jax.nn.silu(pre_act).astype(jnp.bfloat16)
    sigmoid_y = jax.nn.sigmoid(pre_act)
    silu_slope = sigmoid_y * (1.0 + pre_act * (1.0 - sigmoid_y))
    pre_grad = (out_grad.astype(jnp.float32) * train_mask.astype(jnp.float32)[:, None] * silu_slope).astype(jnp.bfloat16)
    wsum = lax.dot_general(aggregated, pre_grad, (((0,), (0,)), ((), ())), preferred_element_type=jnp.float32)
    weight_step = wsum / jnp.sqrt(jnp.mean(wsum * wsum) + 1e-06)
    agg_grad = lax.dot_general(pre_grad, weight, (((1,), (1,)), ((), ())), preferred_element_type=jnp.float32).astype(jnp.bfloat16)

    def backward_row(carry, tile_row):
        adj_block = adj_tiles[tile_row].astype(jnp.float32) * live_mask[tile_row][:, :, None, None]
        row_grads = lax.dynamic_slice_in_dim(agg_grad, tile_row * TILE, TILE, 0).astype(jnp.float32)
        contrib = jnp.einsum('jkab,ad->jkbd', adj_block, row_grads)
        carry = carry.at[group_index, tile_cols[tile_row]].add(contrib)
        return (carry, None)
    start_grad = jnp.zeros((N_REP, TC, TILE, D), jnp.float32)
    group_grad, unused_out = lax.scan(backward_row, start_grad, tile_index)
    feat_grad = group_grad.reshape(N_REP, N_ROWS, NODE_DEV, D).transpose(1, 0, 2, 3).reshape(NODES, D).astype(jnp.bfloat16)
    return (activations, feat_grad, weight_step)
```

```python
import functools

import jax
import jax.numpy as jnp
from jax import lax
from jax.experimental import pallas as pl
from jax.experimental.pallas import tpu as pltpu
from jax.sharding import PartitionSpec as P

MESH = pl.DeviceIdType.MESH
F32 = jnp.float32
BF16 = jnp.bfloat16
INNER = 4


def layer_kernel(
    n_rows, n_rep,
    feat_ref, weight_ref, adj_ref, cols_ref, counts_ref, grad_ref, mask_ref,
    act_ref, fgrad_ref, wstep_ref,
    panel, dense, dense_t, mask_col, part, part_in, grads, w_full, w_out, w_in,
    w_mine, w_all, terms, first_in, second_out, second_in,
    ag_send, ag_recv, part_send, part_recv, grads_send, grads_recv,
    w_send, w_recv, wa_send, wa_recv, first_send, first_recv, second_send, second_recv,
):
    n_dev = n_rows * n_rep
    nodes, width = feat_ref.shape
    tile_rows, slots, tile = adj_ref.shape[0], adj_ref.shape[2], adj_ref.shape[3]
    piece = w_out.shape[1]
    half = w_out.shape[2]
    outer_count = n_rows // INNER
    row = lax.axis_index("rows")
    rep = lax.axis_index("rep")
    me = row * n_rep + rep
    outer, inner = row // INNER, row % INNER
    iy, ix = inner // 2, inner % 2
    inner_peers = [iy * 2 + (1 - ix), (1 - iy) * 2 + ix, (1 - iy) * 2 + (1 - ix)]
    outer_peers = [(outer + d) % outer_count for d in range(1, outer_count)]
    rep_peers = [(rep + d) % n_rep for d in range(1, n_rep)]
    pending = []

    def remote(src, dst, send, recv, row_to, rep_to):
        return pltpu.make_async_remote_copy(
            src_ref=src, dst_ref=dst, send_sem=send, recv_sem=recv,
            device_id=(row_to, rep_to), device_id_type=MESH,
        )

    def post(*spec):
        copy = remote(*spec)
        copy.start()
        pending.append(copy)

    barrier = pltpu.get_barrier_semaphore()

    def greet(d, carry):
        other = (me + d) % n_dev
        pl.semaphore_signal(
            barrier, inc=1, device_id=(other // n_rep, other % n_rep), device_id_type=MESH
        )
        return carry

    lax.fori_loop(1, n_dev, greet, 0)
    pl.semaphore_wait(barrier, n_dev - 1)

    ag_count = 0
    for o in outer_peers:
        post(feat_ref, panel.at[row], ag_send.at[ag_count], ag_recv.at[row], o * INNER + inner, rep)
        ag_count += 1
    for i in inner_peers:
        post(feat_ref, panel.at[row], ag_send.at[ag_count], ag_recv.at[row], outer * INNER + i, rep)
        ag_count += 1
    panel[row] = feat_ref[...]

    def build(r):
        def column(c, carry):
            total = jnp.zeros((tile, tile), F32)
            for k in range(slots):
                chosen = jnp.logical_and(cols_ref[r * slots + k] == c, k < counts_ref[r])
                total = total + jnp.where(chosen, 1.0, 0.0) * adj_ref[r, 0, k].astype(F32)
            at = pl.multiple_of(c * tile, tile)
            dense[r * tile:(r + 1) * tile, pl.ds(at, tile)] = total.astype(BF16)
            dense_t[pl.ds(at, tile), r * tile:(r + 1) * tile] = total.T.astype(BF16)
            return carry

        lax.fori_loop(0, n_rows, column, 0)

    build(0)
    for o in outer_peers:
        source = o * INNER + inner
        block = panel.at[source]
        remote(feat_ref, block, ag_send.at[0], ag_recv.at[source], source, rep).wait_recv()
        for i in inner_peers:
            post(block, block, ag_send.at[ag_count], ag_recv.at[source], outer * INNER + i, rep)
            ag_count += 1
    for r in range(1, tile_rows):
        build(r)
    mask_row = jnp.broadcast_to(mask_ref[...].astype(F32), (nodes, nodes))
    mask_col[...] = mask_row.T
    for i in inner_peers:
        for o in [outer] + outer_peers:
            source = o * INNER + i
            remote(feat_ref, panel.at[source], ag_send.at[0], ag_recv.at[source], source, rep).wait_recv()

    def partial_of(p):
        at = pl.multiple_of(p * nodes, nodes)
        return jnp.dot(
            dense[pl.ds(at, nodes), :], panel[...].reshape(n_rows * nodes, width),
            preferred_element_type=F32,
        )

    for d, p in enumerate(rep_peers):
        part[p] = partial_of(p)
        post(part.at[p], part_in.at[rep], part_send.at[d], part_recv.at[rep], row, p)
    total = partial_of(rep)
    for p in rep_peers:
        remote(part.at[p], part_in.at[p], part_send.at[0], part_recv.at[p], row, p).wait_recv()
        total = total + part_in[p]
    aggregated = total.astype(BF16)
    pre_act = jnp.dot(aggregated, weight_ref[...], preferred_element_type=F32)
    sigmoid = jax.nn.sigmoid(pre_act)
    mask = jnp.concatenate([mask_col[...]] * (width // nodes), axis=1)
    slope = sigmoid * (1.0 + pre_act * (1.0 - sigmoid))
    pre_grad = (grad_ref[...].astype(F32) * mask * slope).astype(BF16)
    grads[rep] = lax.dot_general(
        pre_grad, weight_ref[...], (((1,), (1,)), ((), ())), preferred_element_type=F32
    ).astype(BF16)
    for d, p in enumerate(rep_peers):
        post(grads.at[rep], grads.at[rep], grads_send.at[d], grads_recv.at[rep], row, p)
    w_full[...] = lax.dot_general(
        aggregated, pre_grad, (((0,), (0,)), ((), ())), preferred_element_type=F32
    )
    act_ref[...] = (pre_act * sigmoid).astype(BF16)

    def rows_of(b):
        return pl.ds(b * piece if isinstance(b, int) else pl.multiple_of(b * piece, piece), piece)

    def halves(action):
        if piece % 8 == 0:
            lax.fori_loop(0, n_dev // 2, action, 0)
        else:
            for b in range(n_dev // 2):
                action(b, 0)

    def cut(b, carry):
        rows_at = rows_of(b)
        w_out[2 * b] = w_full[rows_at, :half].astype(w_out.dtype)
        w_out[2 * b + 1] = w_full[rows_at, half:].astype(w_out.dtype)
        return carry

    halves(cut)

    def w_copy(d):
        to = (me + d) % n_dev
        return remote(w_out.at[to], w_in.at[me], w_send.at[d], w_recv.at[me], to // n_rep, to % n_rep)

    def w_copy_in(d):
        to = (me + d) % n_dev
        return remote(w_mine, w_in.at[to], w_send.at[d], w_recv.at[to], to // n_rep, to % n_rep)

    def wa_copy(d):
        to = (me + d) % n_dev
        return remote(w_mine, w_all.at[me], wa_send.at[d], wa_recv.at[me], to // n_rep, to % n_rep)

    def wa_copy_in(d):
        to = (me + d) % n_dev
        return remote(w_mine, w_all.at[to], wa_send.at[d], wa_recv.at[to], to // n_rep, to % n_rep)

    def each(action):
        def step(d, carry):
            action(d)
            return carry

        lax.fori_loop(1, n_dev, step, 0)

    each(lambda d: w_copy(d).start())
    w_in[me] = w_out[me]

    for p in rep_peers:
        remote(grads.at[p], grads.at[p], grads_send.at[0], grads_recv.at[p], row, p).wait_recv()
    row_grads = grads[...].reshape(n_rep * nodes, width)

    def term_of(c):
        at = pl.multiple_of(c * nodes, nodes)
        return jnp.dot(dense_t[pl.ds(at, nodes), :], row_grads, preferred_element_type=F32)

    for d, o in enumerate(outer_peers + [outer]):
        for e, i in enumerate(inner_peers):
            c = o * INNER + i
            terms[c] = term_of(c).astype(BF16)
            slot = inner * outer_count + o
            post(
                terms.at[c], first_in.at[slot], first_send.at[d * (INNER - 1) + e],
                first_recv.at[slot], outer * INNER + i, rep,
            )
    own_terms = [term_of(o * INNER + inner) for o in outer_peers + [outer]]

    each(lambda d: w_copy_in(d).wait_recv())
    w_mine[...] = jnp.sum(w_in[...].astype(F32), axis=0).astype(w_mine.dtype)
    each(lambda d: wa_copy(d).start())
    w_all[me] = w_mine[...]

    for d, o in enumerate(outer_peers + [outer]):
        total = own_terms[d]
        for i in inner_peers:
            slot = i * outer_count + o
            remote(
                terms.at[0], first_in.at[slot], first_send.at[0], first_recv.at[slot],
                outer * INNER + i, rep,
            ).wait_recv()
            total = total + first_in[slot].astype(F32)
        if d < outer_count - 1:
            second_out[d] = total.astype(BF16)
            post(
                second_out.at[d], second_in.at[outer], second_send.at[d],
                second_recv.at[outer], o * INNER + inner, rep,
            )

    each(lambda d: wa_copy_in(d).wait_recv())
    whole = w_all[...].astype(F32)
    scale = lax.rsqrt(jnp.sum(whole * whole) / (width * width) + 1e-06)

    def paste(b, carry):
        rows_at = rows_of(b)
        wstep_ref[rows_at, :half] = w_all[2 * b].astype(F32) * scale
        wstep_ref[rows_at, half:] = w_all[2 * b + 1].astype(F32) * scale
        return carry

    halves(paste)

    for o in outer_peers:
        remote(
            terms.at[0], second_in.at[o], second_send.at[0], second_recv.at[o],
            o * INNER + inner, rep,
        ).wait_recv()
        total = total + second_in[o].astype(F32)
    fgrad_ref[...] = total.astype(BF16)

    for copy in pending:
        copy.wait_send()
    each(lambda d: w_copy(d).wait_send())
    each(lambda d: wa_copy(d).wait_send())


def body(n_rows, n_rep, features, weight, adj_tiles, tile_cols, tile_counts, out_grad, train_mask):
    nodes, width = features.shape
    tile_rows, tile = adj_tiles.shape[0], adj_tiles.shape[-1]
    n_dev = n_rows * n_rep
    outer_count = n_rows // INNER
    piece = 2 * width // n_dev
    half = width // 2
    w_type = BF16 if piece % 16 == 0 else F32
    vmem = pl.BlockSpec(memory_space=pltpu.VMEM)
    smem = pl.BlockSpec(memory_space=pltpu.SMEM)
    dma = pltpu.SemaphoreType.DMA
    block = (nodes, width)
    return pl.pallas_call(
        functools.partial(layer_kernel, n_rows, n_rep),
        out_shape=(
            jax.ShapeDtypeStruct(block, BF16),
            jax.ShapeDtypeStruct(block, BF16),
            jax.ShapeDtypeStruct((width, width), F32),
        ),
        in_specs=[vmem, vmem, vmem, smem, smem, vmem, vmem],
        out_specs=(vmem, vmem, vmem),
        scratch_shapes=[
            pltpu.VMEM((n_rows,) + block, BF16),
            pltpu.VMEM((tile_rows * tile, n_rows * tile), BF16),
            pltpu.VMEM((n_rows * tile, tile_rows * tile), BF16),
            pltpu.VMEM((nodes, nodes), F32),
            pltpu.VMEM((n_rep,) + block, F32),
            pltpu.VMEM((n_rep,) + block, F32),
            pltpu.VMEM((n_rep,) + block, BF16),
            pltpu.VMEM((width, width), F32),
            pltpu.VMEM((n_dev, piece, half), w_type),
            pltpu.VMEM((n_dev, piece, half), w_type),
            pltpu.VMEM((piece, half), w_type),
            pltpu.VMEM((n_dev, piece, half), w_type),
            pltpu.VMEM((n_rows,) + block, BF16),
            pltpu.VMEM((n_rows,) + block, BF16),
            pltpu.VMEM((outer_count,) + block, BF16),
            pltpu.VMEM((outer_count,) + block, BF16),
            dma((n_rows,)), dma((n_rows,)),
            dma((n_rep,)), dma((n_rep,)),
            dma((n_rep,)), dma((n_rep,)),
            dma((n_dev,)), dma((n_dev,)),
            dma((n_dev,)), dma((n_dev,)),
            dma((n_rows,)), dma((n_rows,)),
            dma((outer_count,)), dma((outer_count,)),
        ],
        compiler_params=pltpu.CompilerParams(
            collective_id=0, has_side_effects=True, vmem_limit_bytes=60 * 1024 * 1024
        ),
    )(
        features, weight, adj_tiles, tile_cols.reshape(-1), tile_counts.reshape(-1),
        out_grad, train_mask.reshape(1, -1),
    )


def solution(mesh):
    placed = (
        P(("rows", "rep"), None),
        P(),
        P("rows", "rep", None, None, None),
        P("rows", "rep", None),
        P("rows", "rep"),
        P(("rows", "rep"), None),
        P(("rows", "rep")),
    )
    return jax.shard_map(
        functools.partial(body, mesh.shape["rows"], mesh.shape["rep"]),
        mesh=mesh,
        in_specs=placed,
        out_specs=(P(("rows", "rep"), None), P(("rows", "rep"), None), P()),
        check_vma=False,
    )
```

```python
import functools

import jax
import jax.numpy as jnp
from jax import lax
from jax.experimental import pallas as pl
from jax.experimental.pallas import tpu as pltpu
from jax.sharding import PartitionSpec as P

MESH = pl.DeviceIdType.MESH
F32 = jnp.float32
BF16 = jnp.bfloat16
INNER = 4


def layer_kernel(
    n_rows, n_rep,
    feat_hbm, weight_hbm, adj_hbm, cols_ref, counts_ref, grad_hbm, mask_hbm,
    act_ref, fgrad_ref, wstep_ref,
    weight_ref, adj_ref, grad_ref, mask_ref,
    panel, dense, dense_t, mask_col, part, part_in, shared, w_full, w_out, w_in,
    w_all, terms, own_half, own_terms, relay_in, first_in, second_out, second_in,
    load_sem, ag_send, ag_recv, relay_recv, part_send, part_recv, grads_send, grads_recv,
    w_send, w_recv, wa_send, wa_recv, swap_send, swap_recv, first_send, relay_sem, first_recv, second_send, second_recv,
):
    nodes, width = feat_hbm.shape
    tile_rows, slots, tile = adj_ref.shape[0], adj_ref.shape[2], adj_ref.shape[3]
    piece = w_out.shape[1]
    half = w_out.shape[2]
    outer_count = n_rows // INNER
    row = lax.axis_index("rows")
    rep = lax.axis_index("rep")
    outer, inner = row // INNER, row % INNER
    iy, ix = inner // 2, inner % 2
    inner_x, inner_y = iy * 2 + (1 - ix), (1 - iy) * 2 + ix
    inner_d = (1 - iy) * 2 + (1 - ix)
    turn = 1 - 2 * (outer // (outer_count // 2))
    outer_peers = [(outer + turn * d + outer_count) % outer_count for d in range(1, outer_count)]
    rep_peers = [(rep + d) % n_rep for d in range(1, n_rep)]
    low, high = pl.ds(0, nodes // 2), pl.ds(nodes // 2, nodes // 2)
    pending = []

    def remote(src, dst, send, recv, row_to, rep_to):
        return pltpu.make_async_remote_copy(
            src_ref=src, dst_ref=dst, send_sem=send, recv_sem=recv,
            device_id=(row_to, rep_to), device_id_type=MESH,
        )

    def post(*spec):
        copy = remote(*spec)
        copy.start()
        pending.append(copy)

    barrier = pltpu.get_barrier_semaphore()

    near = [(o * INNER + inner, rep) for o in outer_peers]
    near += [(outer * INNER + i, rep) for i in (inner_x, inner_y)]
    near += [(row, p) for p in rep_peers]
    for other in near:
        pl.semaphore_signal(barrier, inc=1, device_id=other, device_id_type=MESH)
    loads = [
        pltpu.make_async_copy(src, dst, load_sem.at[n])
        for n, (src, dst) in enumerate([
            (adj_hbm, adj_ref), (feat_hbm, panel.at[row]), (mask_hbm, mask_ref),
            (weight_hbm, weight_ref), (grad_hbm, grad_ref),
        ])
    ]
    for load in loads:
        load.start()
    pl.semaphore_wait(barrier, len(near))

    counter = iter(range(2 * n_rows))

    def gather(src, source, rows_at, recv, row_to):
        post(src, panel.at[source, rows_at], ag_send.at[next(counter)], recv.at[source], row_to, rep)

    def gathered(source, rows_at, recv):
        remote(
            panel.at[source, rows_at], panel.at[source, rows_at], ag_send.at[0], recv.at[source],
            outer * INNER + inner_x, rep,
        ).wait_recv()

    full = pl.ds(0, nodes)
    plane_x, plane_y = outer * INNER + inner_x, outer * INNER + inner_y
    for o in outer_peers:
        gather(feat_hbm, row, full, ag_recv, o * INNER + inner)
    gather(feat_hbm, row, full, ag_recv, plane_x)
    gather(feat_hbm, row, full, ag_recv, plane_y)
    loads[0].wait()

    def build(r, start, stop):
        def column(c, carry):
            total = jnp.zeros((tile, tile), F32)
            for k in range(slots):
                chosen = jnp.logical_and(cols_ref[r, 0, k] == c, k < counts_ref[r, 0])
                total = total + jnp.where(chosen, 1.0, 0.0) * adj_ref[r, 0, k].astype(F32)
            at = pl.multiple_of(c * tile, tile)
            dense[r * tile:(r + 1) * tile, pl.ds(at, tile)] = total.astype(BF16)
            dense_t[pl.ds(at, tile), r * tile:(r + 1) * tile] = total.T.astype(BF16)
            return carry

        lax.fori_loop(start, stop, column, 0)

    steps = [outer] + outer_peers
    jobs = [(r, c, c + n_rows // 4) for r in range(tile_rows) for c in range(0, n_rows, n_rows // 4)]
    shares = [len(jobs) * n // (2 * outer_count) for n in range(2 * outer_count + 1)]
    for n, o in enumerate(steps):
        for job in jobs[shares[2 * n]:shares[2 * n + 1]]:
            build(*job)
        if n > 0:
            source = o * INNER + inner
            gathered(source, full, ag_recv)
            gather(panel.at[source], source, full, ag_recv, plane_x)
            gather(panel.at[source], source, full, ag_recv, plane_y)
        for job in jobs[shares[2 * n + 1]:shares[2 * n + 2]]:
            build(*job)
        for before in ([steps[n - 1]] if n > 0 else []) + ([o] if n == outer_count - 1 else []):
            source = before * INNER + inner_x
            gathered(source, full, ag_recv)
            gather(panel.at[source, low], source, low, ag_recv, plane_y)
            source = before * INNER + inner_y
            gathered(source, full, ag_recv)
            gather(panel.at[source, high], source, high, relay_recv, plane_x)
    for load in loads[1:]:
        load.wait()
    mask_row = jnp.broadcast_to(mask_ref[...].astype(F32), (nodes, nodes))
    mask_col[...] = mask_row.T
    for o in steps:
        gathered(o * INNER + inner_d, low, ag_recv)
        gathered(o * INNER + inner_d, high, relay_recv)

    def partial_of(p):
        at = pl.multiple_of(p * nodes, nodes)
        return jnp.dot(
            dense[pl.ds(at, nodes), :], panel[...].reshape(n_rows * nodes, width),
            preferred_element_type=F32,
        )

    for d, p in enumerate(rep_peers):
        part[p] = partial_of(p)
        post(part.at[p], part_in.at[rep], part_send.at[d], part_recv.at[rep], row, p)
    total = partial_of(rep)
    for p in rep_peers:
        remote(part.at[p], part_in.at[p], part_send.at[0], part_recv.at[p], row, p).wait_recv()
        total = total + part_in[p]
    aggregated = total.astype(BF16)
    shared[0, rep] = aggregated
    for d, p in enumerate(rep_peers):
        post(shared.at[0, rep], shared.at[0, rep], grads_send.at[0, d], grads_recv.at[0, rep], row, p)
    pre_act = jnp.dot(aggregated, weight_ref[...], preferred_element_type=F32)
    sigmoid = jax.nn.sigmoid(pre_act)
    mask = jnp.concatenate([mask_col[...]] * (width // nodes), axis=1)
    slope = sigmoid * (1.0 + pre_act * (1.0 - sigmoid))
    pre_grad = (grad_ref[...].astype(F32) * mask * slope).astype(BF16)
    shared[1, rep] = pre_grad
    for d, p in enumerate(rep_peers):
        post(shared.at[1, rep], shared.at[1, rep], grads_send.at[1, d], grads_recv.at[1, rep], row, p)
    act_ref[...] = (pre_act * sigmoid).astype(BF16)

    for n in range(2):
        for p in rep_peers:
            remote(shared.at[n, p], shared.at[n, p], grads_send.at[0, 0], grads_recv.at[n, p], row, p).wait_recv()
    row_pre_grads = shared[1].reshape(n_rep * nodes, width)
    row_grads = lax.dot_general(
        row_pre_grads, weight_ref[...], (((1,), (1,)), ((), ())), preferred_element_type=F32
    ).astype(BF16)

    def term_of(c):
        at = pl.multiple_of(c * nodes, nodes)
        return jnp.dot(dense_t[pl.ds(at, nodes), :], row_grads, preferred_element_type=F32)

    order = outer_peers[::-1] + [outer]
    counter_first = iter(range(6 * outer_count))

    def give(src, dst, recv, row_to):
        post(src, dst, first_send.at[next(counter_first)], recv, row_to, rep)

    def taken(dst, recv):
        remote(dst, dst, first_send.at[0], recv, plane_x, rep).wait_recv()

    def first_step(o):
        c = o * INNER + inner_d
        terms[c] = term_of(c).astype(BF16)
        give(terms.at[c, low], relay_in.at[0, o], relay_sem.at[0, o], plane_x)
        give(terms.at[c, high], relay_in.at[1, o], relay_sem.at[1, o], plane_y)
        for way, i, plane in ((0, inner_y, plane_y), (1, inner_x, plane_x)):
            c = o * INNER + i
            value = term_of(c)
            top, bottom = value[:nodes // 2], value[nodes // 2:]
            ready, kept = (bottom, top) if way == 0 else (top, bottom)
            at = high if way == 0 else low
            terms[c, at] = ready.astype(BF16)
            give(terms.at[c, at], first_in.at[way, o, at], first_recv.at[2 * way, o], plane)
            own_half[way, o] = kept
        own_terms[o] = term_of(o * INNER + inner)

    def second_step(o):
        for way, i, plane in ((0, inner_y, plane_y), (1, inner_x, plane_x)):
            c = o * INNER + i
            at = low if way == 0 else high
            taken(relay_in.at[way, o], relay_sem.at[way, o])
            terms[c, at] = (own_half[way, o] + relay_in[way, o].astype(F32)).astype(BF16)
            give(terms.at[c, at], first_in.at[way, o, at], first_recv.at[2 * way + 1, o], plane)

    def third_step(d, o):
        for way in range(2):
            for stage in range(2):
                at = low if (way == 0) == (stage == 1) else high
                taken(first_in.at[way, o, at], first_recv.at[2 * way + stage, o])
        total = own_terms[o] + first_in[0, o].astype(F32) + first_in[1, o].astype(F32)
        if d < outer_count - 1:
            second_out[d] = total.astype(BF16)
            post(
                second_out.at[d], second_in.at[outer], second_send.at[d],
                second_recv.at[outer], o * INNER + inner, rep,
            )
        return total

    def w_send_terms():
        column = pl.multiple_of((rep % 2) * half, half)
        w_full[...] = lax.dot_general(
            shared[0].reshape(n_rep * nodes, width), row_pre_grads,
            (((0,), (0,)), ((), ())), preferred_element_type=F32,
        )
        w_half = w_full[:, pl.ds(column, half)]
        for b in range(n_rows):
            w_out[b] = w_half[b * piece:(b + 1) * piece].astype(w_out.dtype)
        for n, to in enumerate(row_peers):
            post(w_out.at[to], w_in.at[row], w_send.at[n], w_recv.at[row], to, rep)
        w_in[row] = w_out[row]

    def w_send_sums():
        for to in row_peers:
            remote(w_out.at[to], w_in.at[to], w_send.at[0], w_recv.at[to], to, rep).wait_recv()
        side = rep % 2
        w_all[side, row] = jnp.sum(w_in[...].astype(F32), axis=0).astype(w_all.dtype)
        for n, to in enumerate(row_peers):
            post(w_all.at[side, row], w_all.at[side, row], wa_send.at[n], wa_recv.at[row], to, rep)

    def w_swap():
        side = rep % 2
        for to in row_peers:
            block = w_all.at[side, to]
            remote(block, block, wa_send.at[0], wa_recv.at[to], to, rep).wait_recv()
        post(w_all.at[side], w_all.at[side], swap_send, swap_recv, row, (rep + 1) % n_rep)

    def w_finish():
        other = w_all.at[(rep + 1) % 2]
        remote(other, other, swap_send, swap_recv, row, (rep + 1) % n_rep).wait_recv()
        whole = w_all[...].astype(F32)
        scale = lax.rsqrt(jnp.sum(whole * whole) / (width * width) + 1e-06)
        for side in range(2):
            for b in range(n_rows):
                wstep_ref[b * piece:(b + 1) * piece, side * half:(side + 1) * half] = whole[side, b] * scale

    row_peers = [(row + d) % n_rows for d in range(1, n_rows)]
    first_step(order[0])
    w_send_terms()
    if outer_count > 1:
        first_step(order[1])
    for d, o in enumerate(order):
        second_step(o)
        if d + 2 < outer_count:
            first_step(order[d + 2])
        if d > 0:
            third_step(d - 1, order[d - 1])
        if d == min(2, outer_count - 1):
            w_send_sums()
    total = third_step(outer_count - 1, outer)
    w_swap()
    w_finish()

    for o in outer_peers:
        remote(
            terms.at[0], second_in.at[o], second_send.at[0], second_recv.at[o],
            o * INNER + inner, rep,
        ).wait_recv()
        total = total + second_in[o].astype(F32)
    fgrad_ref[...] = total.astype(BF16)

    for copy in pending:
        copy.wait_send()


def body(n_rows, n_rep, features, weight, adj_tiles, tile_cols, tile_counts, out_grad, train_mask):
    nodes, width = features.shape
    tile_rows, tile = adj_tiles.shape[0], adj_tiles.shape[-1]
    outer_count = n_rows // INNER
    piece = width // n_rows
    half = width // 2
    w_type = BF16 if piece % 16 == 0 else F32
    vmem = pl.BlockSpec(memory_space=pltpu.VMEM)
    smem = pl.BlockSpec(memory_space=pltpu.SMEM)
    hbm = pl.BlockSpec(memory_space=pltpu.HBM)
    half_block = (nodes // 2, width)
    dma = pltpu.SemaphoreType.DMA
    vmem_bytes = (62 if n_rows <= 16 else 63) * 1024 * 1024
    block = (nodes, width)
    return pl.pallas_call(
        functools.partial(layer_kernel, n_rows, n_rep),
        out_shape=(
            jax.ShapeDtypeStruct(block, BF16),
            jax.ShapeDtypeStruct(block, BF16),
            jax.ShapeDtypeStruct((width, width), F32),
        ),
        in_specs=[hbm, hbm, hbm, smem, smem, hbm, hbm],
        out_specs=(vmem, vmem, vmem),
        scratch_shapes=[
            pltpu.VMEM(weight.shape, BF16),
            pltpu.VMEM(adj_tiles.shape, BF16),
            pltpu.VMEM(block, BF16),
            pltpu.VMEM((1, nodes), jnp.int32),
            pltpu.VMEM((n_rows,) + block, BF16),
            pltpu.VMEM((tile_rows * tile, n_rows * tile), BF16),
            pltpu.VMEM((n_rows * tile, tile_rows * tile), BF16),
            pltpu.VMEM((nodes, nodes), F32),
            pltpu.VMEM((n_rep,) + block, F32),
            pltpu.VMEM((n_rep,) + block, F32),
            pltpu.VMEM((2, n_rep) + block, BF16),
            pltpu.VMEM((width, width), F32),
            pltpu.VMEM((n_rows, piece, half), w_type),
            pltpu.VMEM((n_rows, piece, half), w_type),
            pltpu.VMEM((2, n_rows, piece, half), w_type),
            pltpu.VMEM((n_rows,) + block, BF16),
            pltpu.VMEM((2, outer_count) + half_block, F32),
            pltpu.VMEM((outer_count,) + block, F32),
            pltpu.VMEM((2, outer_count) + half_block, BF16),
            pltpu.VMEM((2, outer_count) + block, BF16),
            pltpu.VMEM((outer_count,) + block, BF16),
            pltpu.VMEM((outer_count,) + block, BF16),
            dma((5,)),
            dma((2 * n_rows,)), dma((n_rows,)), dma((n_rows,)),
            dma((n_rep,)), dma((n_rep,)),
            dma((2, n_rep)), dma((2, n_rep)),
            dma((n_rows,)), dma((n_rows,)),
            dma((n_rows,)), dma((n_rows,)),
            dma, dma,
            dma((6 * outer_count,)), dma((2, outer_count)), dma((4, outer_count)),
            dma((outer_count,)), dma((outer_count,)),
        ],
        compiler_params=pltpu.CompilerParams(
            collective_id=0, has_side_effects=True, vmem_limit_bytes=vmem_bytes
        ),
    )(
        features, weight, adj_tiles, tile_cols, tile_counts,
        out_grad, train_mask.reshape(1, -1),
    )
def solution(mesh):
    placed = (
        P(("rows", "rep"), None),
        P(),
        P("rows", "rep", None, None, None),
        P("rows", "rep", None),
        P("rows", "rep"),
        P(("rows", "rep"), None),
        P(("rows", "rep")),
    )
    return jax.shard_map(
        functools.partial(body, mesh.shape["rows"], mesh.shape["rep"]),
        mesh=mesh,
        in_specs=placed,
        out_specs=(P(("rows", "rep"), None), P(("rows", "rep"), None), P()),
        check_vma=False,
    )
```

```python
import functools

import jax
import jax.numpy as jnp
from jax import lax
from jax.experimental import pallas as pl
from jax.experimental.pallas import tpu as pltpu
from jax.sharding import PartitionSpec as P

MESH = pl.DeviceIdType.MESH
F32 = jnp.float32
BF16 = jnp.bfloat16
INNER = 4


def layer_kernel(
    n_rows, n_rep,
    feat_hbm, weight_hbm, adj_hbm, cols_ref, counts_ref, grad_hbm, mask_hbm,
    act_ref, fgrad_ref, wstep_ref,
    weight_ref, adj_ref, grad_ref, mask_ref,
    panel, dense, dense_t, mask_col, part, part_in, shared, w_full, w_out, w_in,
    w_all, terms, own_half, own_terms, relay_in, first_in, second_out, second_in,
    load_sem, ag_send, ag_recv, relay_recv, part_send, part_recv, grads_send, grads_recv,
    w_send, w_recv, wa_send, wa_recv, swap_send, swap_recv, first_send, relay_sem, first_recv, second_send, second_recv,
):
    nodes, width = feat_hbm.shape
    tile_rows, slots, tile = adj_ref.shape[0], adj_ref.shape[2], adj_ref.shape[3]
    piece = w_out.shape[1]
    half = w_out.shape[2]
    outer_count = n_rows // INNER
    row = lax.axis_index("rows")
    rep = lax.axis_index("rep")
    outer, inner = row // INNER, row % INNER
    iy, ix = inner // 2, inner % 2
    inner_x, inner_y = iy * 2 + (1 - ix), (1 - iy) * 2 + ix
    inner_d = (1 - iy) * 2 + (1 - ix)
    turn = 1 - 2 * (outer // (outer_count // 2))
    outer_peers = [(outer + turn * d + outer_count) % outer_count for d in range(1, outer_count)]
    rep_peers = [(rep + d) % n_rep for d in range(1, n_rep)]
    low, high = pl.ds(0, nodes // 2), pl.ds(nodes // 2, nodes // 2)
    pending = []

    def remote(src, dst, send, recv, row_to, rep_to):
        return pltpu.make_async_remote_copy(
            src_ref=src, dst_ref=dst, send_sem=send, recv_sem=recv,
            device_id=(row_to, rep_to), device_id_type=MESH,
        )

    def post(*spec):
        copy = remote(*spec)
        copy.start()
        pending.append(copy)

    barrier = pltpu.get_barrier_semaphore()

    near = [(o * INNER + inner, rep) for o in outer_peers]
    near += [(outer * INNER + i, rep) for i in (inner_x, inner_y)]
    near += [(row, p) for p in rep_peers]
    for other in near:
        pl.semaphore_signal(barrier, inc=1, device_id=other, device_id_type=MESH)
    loads = [
        pltpu.make_async_copy(src, dst, load_sem.at[n])
        for n, (src, dst) in enumerate([
            (adj_hbm, adj_ref), (feat_hbm, panel.at[row]), (mask_hbm, mask_ref),
            (weight_hbm, weight_ref), (grad_hbm, grad_ref),
        ])
    ]
    for load in loads:
        load.start()
    pl.semaphore_wait(barrier, len(near))

    counter = iter(range(2 * n_rows))

    def gather(src, source, rows_at, recv, row_to):
        post(src, panel.at[source, rows_at], ag_send.at[next(counter)], recv.at[source], row_to, rep)

    def gathered(source, rows_at, recv):
        remote(
            panel.at[source, rows_at], panel.at[source, rows_at], ag_send.at[0], recv.at[source],
            outer * INNER + inner_x, rep,
        ).wait_recv()

    full = pl.ds(0, nodes)
    plane_x, plane_y = outer * INNER + inner_x, outer * INNER + inner_y
    for o in outer_peers:
        gather(feat_hbm, row, full, ag_recv, o * INNER + inner)
    gather(feat_hbm, row, full, ag_recv, plane_x)
    gather(feat_hbm, row, full, ag_recv, plane_y)
    loads[0].wait()

    def build(r, start, stop):
        def column(c, carry):
            total = jnp.zeros((tile, tile), F32)
            for k in range(slots):
                chosen = jnp.logical_and(cols_ref[r, 0, k] == c, k < counts_ref[r])
                total = total + jnp.where(chosen, 1.0, 0.0) * adj_ref[r, 0, k].astype(F32)
            at = pl.multiple_of(c * tile, tile)
            dense[r * tile:(r + 1) * tile, pl.ds(at, tile)] = total.astype(BF16)
            dense_t[pl.ds(at, tile), r * tile:(r + 1) * tile] = total.T.astype(BF16)
            return carry

        lax.fori_loop(start, stop, column, 0)

    steps = [outer] + outer_peers
    jobs = [(r, c, c + n_rows // 4) for r in range(tile_rows) for c in range(0, n_rows, n_rows // 4)]
    shares = [len(jobs) * n // (2 * outer_count) for n in range(2 * outer_count + 1)]
    for n, o in enumerate(steps):
        for job in jobs[shares[2 * n]:shares[2 * n + 1]]:
            build(*job)
        if n > 0:
            source = o * INNER + inner
            gathered(source, full, ag_recv)
            gather(panel.at[source], source, full, ag_recv, plane_x)
            gather(panel.at[source], source, full, ag_recv, plane_y)
        for job in jobs[shares[2 * n + 1]:shares[2 * n + 2]]:
            build(*job)
        for before in ([steps[n - 1]] if n > 0 else []) + ([o] if n == outer_count - 1 else []):
            source = before * INNER + inner_x
            gathered(source, full, ag_recv)
            gather(panel.at[source, low], source, low, ag_recv, plane_y)
            source = before * INNER + inner_y
            gathered(source, full, ag_recv)
            gather(panel.at[source, high], source, high, relay_recv, plane_x)
    for load in loads[1:]:
        load.wait()
    mask_row = jnp.broadcast_to(mask_ref[...].astype(F32), (nodes, nodes))
    mask_col[...] = mask_row.T
    for o in steps:
        gathered(o * INNER + inner_d, low, ag_recv)
        gathered(o * INNER + inner_d, high, relay_recv)

    def partial_of(p):
        at = pl.multiple_of(p * nodes, nodes)
        return jnp.dot(
            dense[pl.ds(at, nodes), :], panel[...].reshape(n_rows * nodes, width),
            preferred_element_type=F32,
        )

    for d, p in enumerate(rep_peers):
        part[p] = partial_of(p)
        post(part.at[p], part_in.at[rep], part_send.at[d], part_recv.at[rep], row, p)
    total = partial_of(rep)
    for p in rep_peers:
        remote(part.at[p], part_in.at[p], part_send.at[0], part_recv.at[p], row, p).wait_recv()
        total = total + part_in[p]
    aggregated = total.astype(BF16)
    shared[0, rep] = aggregated
    for d, p in enumerate(rep_peers):
        post(shared.at[0, rep], shared.at[0, rep], grads_send.at[0, d], grads_recv.at[0, rep], row, p)
    pre_act = jnp.dot(aggregated, weight_ref[...], preferred_element_type=F32)
    sigmoid = jax.nn.sigmoid(pre_act)
    mask = jnp.concatenate([mask_col[...]] * (width // nodes), axis=1)
    slope = sigmoid * (1.0 + pre_act * (1.0 - sigmoid))
    pre_grad = (grad_ref[...].astype(F32) * mask * slope).astype(BF16)
    shared[1, rep] = pre_grad
    for d, p in enumerate(rep_peers):
        post(shared.at[1, rep], shared.at[1, rep], grads_send.at[1, d], grads_recv.at[1, rep], row, p)
    act_ref[...] = (pre_act * sigmoid).astype(BF16)

    for n in range(2):
        for p in rep_peers:
            remote(shared.at[n, p], shared.at[n, p], grads_send.at[0, 0], grads_recv.at[n, p], row, p).wait_recv()
    row_pre_grads = shared[1].reshape(n_rep * nodes, width)
    row_grads = lax.dot_general(
        row_pre_grads, weight_ref[...], (((1,), (1,)), ((), ())), preferred_element_type=F32
    ).astype(BF16)

    def term_of(c):
        at = pl.multiple_of(c * nodes, nodes)
        return jnp.dot(dense_t[pl.ds(at, nodes), :], row_grads, preferred_element_type=F32)

    order = outer_peers[::-1] + [outer]
    counter_first = iter(range(6 * outer_count))

    def give(src, dst, recv, row_to):
        post(src, dst, first_send.at[next(counter_first)], recv, row_to, rep)

    def taken(dst, recv):
        remote(dst, dst, first_send.at[0], recv, plane_x, rep).wait_recv()

    def first_step(o):
        c = o * INNER + inner_d
        terms[c] = term_of(c).astype(BF16)
        give(terms.at[c, low], relay_in.at[0, o], relay_sem.at[0, o], plane_x)
        give(terms.at[c, high], relay_in.at[1, o], relay_sem.at[1, o], plane_y)
        for way, i, plane in ((0, inner_y, plane_y), (1, inner_x, plane_x)):
            c = o * INNER + i
            value = term_of(c)
            top, bottom = value[:nodes // 2], value[nodes // 2:]
            ready, kept = (bottom, top) if way == 0 else (top, bottom)
            at = high if way == 0 else low
            terms[c, at] = ready.astype(BF16)
            give(terms.at[c, at], first_in.at[way, o, at], first_recv.at[2 * way, o], plane)
            own_half[way, o] = kept
        own_terms[o] = term_of(o * INNER + inner)

    def second_step(o):
        for way, i, plane in ((0, inner_y, plane_y), (1, inner_x, plane_x)):
            c = o * INNER + i
            at = low if way == 0 else high
            taken(relay_in.at[way, o], relay_sem.at[way, o])
            terms[c, at] = (own_half[way, o] + relay_in[way, o].astype(F32)).astype(BF16)
            give(terms.at[c, at], first_in.at[way, o, at], first_recv.at[2 * way + 1, o], plane)

    def third_step(d, o):
        for way in range(2):
            for stage in range(2):
                at = low if (way == 0) == (stage == 1) else high
                taken(first_in.at[way, o, at], first_recv.at[2 * way + stage, o])
        total = own_terms[o] + first_in[0, o].astype(F32) + first_in[1, o].astype(F32)
        if d < outer_count - 1:
            second_out[d] = total.astype(BF16)
            post(
                second_out.at[d], second_in.at[outer], second_send.at[d],
                second_recv.at[outer], o * INNER + inner, rep,
            )
        return total

    def w_send_terms():
        column = pl.multiple_of((rep % 2) * half, half)
        w_full[...] = lax.dot_general(
            shared[0].reshape(n_rep * nodes, width), row_pre_grads,
            (((0,), (0,)), ((), ())), preferred_element_type=F32,
        )
        w_half = w_full[:, pl.ds(column, half)]
        for b in range(n_rows):
            w_out[b] = w_half[b * piece:(b + 1) * piece].astype(w_out.dtype)
        for n, to in enumerate(row_peers):
            post(w_out.at[to], w_in.at[row], w_send.at[n], w_recv.at[row], to, rep)
        w_in[row] = w_out[row]

    def w_send_sums():
        for to in row_peers:
            remote(w_out.at[to], w_in.at[to], w_send.at[0], w_recv.at[to], to, rep).wait_recv()
        side = rep % 2
        w_all[side, row] = jnp.sum(w_in[...].astype(F32), axis=0).astype(w_all.dtype)
        for n, to in enumerate(row_peers):
            post(w_all.at[side, row], w_all.at[side, row], wa_send.at[n], wa_recv.at[row], to, rep)

    def w_swap():
        side = rep % 2
        for to in row_peers:
            block = w_all.at[side, to]
            remote(block, block, wa_send.at[0], wa_recv.at[to], to, rep).wait_recv()
        post(w_all.at[side], w_all.at[side], swap_send, swap_recv, row, (rep + 1) % n_rep)

    def w_finish():
        other = w_all.at[(rep + 1) % 2]
        remote(other, other, swap_send, swap_recv, row, (rep + 1) % n_rep).wait_recv()
        whole = w_all[...].astype(F32)
        scale = lax.rsqrt(jnp.sum(whole * whole) / (width * width) + 1e-06)
        for side in range(2):
            for b in range(n_rows):
                wstep_ref[b * piece:(b + 1) * piece, side * half:(side + 1) * half] = whole[side, b] * scale

    row_peers = [(row + d) % n_rows for d in range(1, n_rows)]
    first_step(order[0])
    w_send_terms()
    if outer_count > 1:
        first_step(order[1])
    for d, o in enumerate(order):
        second_step(o)
        if d + 2 < outer_count:
            first_step(order[d + 2])
        if d > 0:
            third_step(d - 1, order[d - 1])
        if d == min(2, outer_count - 1):
            w_send_sums()
    total = third_step(outer_count - 1, outer)
    w_swap()
    w_finish()

    for o in outer_peers:
        remote(
            terms.at[0], second_in.at[o], second_send.at[0], second_recv.at[o],
            o * INNER + inner, rep,
        ).wait_recv()
        total = total + second_in[o].astype(F32)
    fgrad_ref[...] = total.astype(BF16)

    for copy in pending:
        copy.wait_send()


def body(n_rows, n_rep, features, weight, adj_tiles, tile_cols, tile_counts, out_grad, train_mask):
    nodes, width = features.shape
    tile_rows, tile = adj_tiles.shape[0], adj_tiles.shape[-1]
    outer_count = n_rows // INNER
    piece = width // n_rows
    half = width // 2
    w_type = BF16 if piece % 16 == 0 else F32
    vmem = pl.BlockSpec(memory_space=pltpu.VMEM)
    smem = pl.BlockSpec(memory_space=pltpu.SMEM)
    hbm = pl.BlockSpec(memory_space=pltpu.HBM)
    half_block = (nodes // 2, width)
    dma = pltpu.SemaphoreType.DMA
    vmem_bytes = int((53.8 if n_rows <= 16 else 63) * 1024 * 1024)
    block = (nodes, width)
    return pl.pallas_call(
        functools.partial(layer_kernel, n_rows, n_rep),
        out_shape=(
            jax.ShapeDtypeStruct(block, BF16),
            jax.ShapeDtypeStruct(block, BF16),
            jax.ShapeDtypeStruct((width, width), F32),
        ),
        in_specs=[hbm, hbm, hbm, smem, smem, hbm, hbm],
        out_specs=(vmem, vmem, vmem),
        scratch_shapes=[
            pltpu.VMEM(weight.shape, BF16),
            pltpu.VMEM(adj_tiles.shape, BF16),
            pltpu.VMEM(block, BF16),
            pltpu.VMEM((1, nodes), jnp.int32),
            pltpu.VMEM((n_rows,) + block, BF16),
            pltpu.VMEM((tile_rows * tile, n_rows * tile), BF16),
            pltpu.VMEM((n_rows * tile, tile_rows * tile), BF16),
            pltpu.VMEM((nodes, nodes), F32),
            pltpu.VMEM((n_rep,) + block, F32),
            pltpu.VMEM((n_rep,) + block, F32),
            pltpu.VMEM((2, n_rep) + block, BF16),
            pltpu.VMEM((width, width), F32),
            pltpu.VMEM((n_rows, piece, half), w_type),
            pltpu.VMEM((n_rows, piece, half), w_type),
            pltpu.VMEM((2, n_rows, piece, half), w_type),
            pltpu.VMEM((n_rows,) + block, BF16),
            pltpu.VMEM((2, outer_count) + half_block, F32),
            pltpu.VMEM((outer_count,) + block, F32),
            pltpu.VMEM((2, outer_count) + half_block, BF16),
            pltpu.VMEM((2, outer_count) + block, BF16),
            pltpu.VMEM((outer_count,) + block, BF16),
            pltpu.VMEM((outer_count,) + block, BF16),
            dma((5,)),
            dma((2 * n_rows,)), dma((n_rows,)), dma((n_rows,)),
            dma((n_rep,)), dma((n_rep,)),
            dma((2, n_rep)), dma((2, n_rep)),
            dma((n_rows,)), dma((n_rows,)),
            dma((n_rows,)), dma((n_rows,)),
            dma, dma,
            dma((6 * outer_count,)), dma((2, outer_count)), dma((4, outer_count)),
            dma((outer_count,)), dma((outer_count,)),
        ],
        compiler_params=pltpu.CompilerParams(
            collective_id=0, has_side_effects=True, vmem_limit_bytes=vmem_bytes
        ),
    )(
        features, weight, adj_tiles, tile_cols, tile_counts.reshape(-1),
        out_grad, train_mask.reshape(1, -1),
    )
def solution(mesh):
    placed = (
        P(("rows", "rep"), None),
        P(),
        P("rows", "rep", None, None, None),
        P("rows", "rep", None),
        P("rows", "rep"),
        P(("rows", "rep"), None),
        P(("rows", "rep")),
    )
    return jax.shard_map(
        functools.partial(body, mesh.shape["rows"], mesh.shape["rep"]),
        mesh=mesh,
        in_specs=placed,
        out_specs=(P(("rows", "rep"), None), P(("rows", "rep"), None), P()),
        check_vma=False,
    )
```

```python
import functools

import jax
import jax.numpy as jnp
from jax import lax
from jax.experimental import pallas as pl
from jax.experimental.pallas import tpu as pltpu
from jax.sharding import PartitionSpec as P

MESH = pl.DeviceIdType.MESH
F32 = jnp.float32
BF16 = jnp.bfloat16
INNER = 4


def layer_kernel(
    n_rows, n_rep,
    feat_hbm, weight_hbm, adj_hbm, cols_ref, counts_ref, grad_hbm, mask_hbm,
    act_ref, fgrad_ref, wstep_ref,
    weight_ref, adj_ref, grad_ref, mask_ref,
    panel, dense, dense_t, mask_col, part, part_in, shared, w_full, w_out, w_in,
    w_all, terms, own_half, own_terms, relay_in, first_in, second_out, second_in,
    load_sem, ag_send, ag_recv, relay_recv, part_send, part_recv, grads_send, grads_recv,
    w_send, w_recv, wa_send, wa_recv, swap_send, swap_recv, first_send, relay_sem, first_recv, second_send, second_recv,
):
    nodes, width = feat_hbm.shape
    tile_rows, slots, tile = adj_ref.shape[0], adj_ref.shape[2], adj_ref.shape[3]
    piece = w_out.shape[1]
    half = w_out.shape[2]
    outer_count = n_rows // INNER
    row = lax.axis_index("rows")
    rep = lax.axis_index("rep")
    outer, inner = row // INNER, row % INNER
    iy, ix = inner // 2, inner % 2
    inner_x, inner_y = iy * 2 + (1 - ix), (1 - iy) * 2 + ix
    inner_d = (1 - iy) * 2 + (1 - ix)
    turn = 1 - 2 * (outer // (outer_count // 2))
    outer_peers = [(outer + turn * d + outer_count) % outer_count for d in range(1, outer_count)]
    rep_peers = [(rep + d) % n_rep for d in range(1, n_rep)]
    low, high = pl.ds(0, nodes // 2), pl.ds(nodes // 2, nodes // 2)
    pending = []

    def remote(src, dst, send, recv, row_to, rep_to):
        return pltpu.make_async_remote_copy(
            src_ref=src, dst_ref=dst, send_sem=send, recv_sem=recv,
            device_id=(row_to, rep_to), device_id_type=MESH,
        )

    def post(*spec):
        copy = remote(*spec)
        copy.start()
        pending.append(copy)

    barrier = pltpu.get_barrier_semaphore()

    near = [(o * INNER + inner, rep) for o in outer_peers]
    near += [(outer * INNER + i, rep) for i in (inner_x, inner_y)]
    near += [(row, p) for p in rep_peers]
    for other in near:
        pl.semaphore_signal(barrier, inc=1, device_id=other, device_id_type=MESH)
    loads = [
        pltpu.make_async_copy(src, dst, load_sem.at[n])
        for n, (src, dst) in enumerate([
            (adj_hbm, adj_ref), (feat_hbm, panel.at[row]), (mask_hbm, mask_ref),
            (weight_hbm, weight_ref), (grad_hbm, grad_ref),
        ])
    ]
    for load in loads:
        load.start()
    pl.semaphore_wait(barrier, len(near))

    counter = iter(range(2 * n_rows))

    def gather(src, source, rows_at, recv, row_to):
        post(src, panel.at[source, rows_at], ag_send.at[next(counter)], recv.at[source], row_to, rep)

    def gathered(source, rows_at, recv):
        remote(
            panel.at[source, rows_at], panel.at[source, rows_at], ag_send.at[0], recv.at[source],
            outer * INNER + inner_x, rep,
        ).wait_recv()

    full = pl.ds(0, nodes)
    plane_x, plane_y = outer * INNER + inner_x, outer * INNER + inner_y
    for o in outer_peers:
        gather(feat_hbm, row, full, ag_recv, o * INNER + inner)
    gather(feat_hbm, row, full, ag_recv, plane_x)
    gather(feat_hbm, row, full, ag_recv, plane_y)
    loads[0].wait()

    def build(r, start, stop):
        def column(c, carry):
            total = jnp.zeros((tile, tile), F32)
            for k in range(slots):
                chosen = jnp.logical_and(cols_ref[r, 0, k] == c, k < counts_ref[r])
                total = total + jnp.where(chosen, 1.0, 0.0) * adj_ref[r, 0, k].astype(F32)
            at = pl.multiple_of(c * tile, tile)
            dense[r * tile:(r + 1) * tile, pl.ds(at, tile)] = total.astype(BF16)
            dense_t[pl.ds(at, tile), r * tile:(r + 1) * tile] = total.T.astype(BF16)
            return carry

        lax.fori_loop(start, stop, column, 0)

    steps = [outer] + outer_peers
    jobs = [(r, c, c + n_rows // 4) for r in range(tile_rows) for c in range(0, n_rows, n_rows // 4)]
    shares = [len(jobs) * n // (2 * outer_count) for n in range(2 * outer_count + 1)]
    for n, o in enumerate(steps):
        for job in jobs[shares[2 * n]:shares[2 * n + 1]]:
            build(*job)
        if n > 0:
            source = o * INNER + inner
            gathered(source, full, ag_recv)
            gather(panel.at[source], source, full, ag_recv, plane_x)
            gather(panel.at[source], source, full, ag_recv, plane_y)
        for job in jobs[shares[2 * n + 1]:shares[2 * n + 2]]:
            build(*job)
        for before in ([steps[n - 1]] if n > 0 else []) + ([o] if n == outer_count - 1 else []):
            source = before * INNER + inner_x
            gathered(source, full, ag_recv)
            gather(panel.at[source, low], source, low, ag_recv, plane_y)
            source = before * INNER + inner_y
            gathered(source, full, ag_recv)
            gather(panel.at[source, high], source, high, relay_recv, plane_x)
    for load in loads[1:]:
        load.wait()
    mask_row = jnp.broadcast_to(mask_ref[...].astype(F32), (nodes, nodes))
    mask_col[...] = mask_row.T
    for o in steps:
        gathered(o * INNER + inner_d, low, ag_recv)
        gathered(o * INNER + inner_d, high, relay_recv)

    def partial_of(p):
        at = pl.multiple_of(p * nodes, nodes)
        return jnp.dot(
            dense[pl.ds(at, nodes), :], panel[...].reshape(n_rows * nodes, width),
            preferred_element_type=F32,
        )

    for d, p in enumerate(rep_peers):
        part[p] = partial_of(p)
        post(part.at[p], part_in.at[rep], part_send.at[d], part_recv.at[rep], row, p)
    total = partial_of(rep)
    for p in rep_peers:
        remote(part.at[p], part_in.at[p], part_send.at[0], part_recv.at[p], row, p).wait_recv()
        total = total + part_in[p]
    aggregated = total.astype(BF16)
    shared[0, rep] = aggregated
    for d, p in enumerate(rep_peers):
        post(shared.at[0, rep], shared.at[0, rep], grads_send.at[0, d], grads_recv.at[0, rep], row, p)
    pre_act = jnp.dot(aggregated, weight_ref[...], preferred_element_type=F32)
    sigmoid = jax.nn.sigmoid(pre_act)
    mask = jnp.concatenate([mask_col[...]] * (width // nodes), axis=1)
    slope = sigmoid * (1.0 + pre_act * (1.0 - sigmoid))
    pre_grad = (grad_ref[...].astype(F32) * mask * slope).astype(BF16)
    shared[1, rep] = pre_grad
    for d, p in enumerate(rep_peers):
        post(shared.at[1, rep], shared.at[1, rep], grads_send.at[1, d], grads_recv.at[1, rep], row, p)
    act_ref[...] = (pre_act * sigmoid).astype(BF16)

    for n in range(2):
        for p in rep_peers:
            remote(shared.at[n, p], shared.at[n, p], grads_send.at[0, 0], grads_recv.at[n, p], row, p).wait_recv()
    row_pre_grads = shared[1].reshape(n_rep * nodes, width)
    row_grads = lax.dot_general(
        row_pre_grads, weight_ref[...], (((1,), (1,)), ((), ())), preferred_element_type=F32
    ).astype(BF16)

    def term_of(c):
        at = pl.multiple_of(c * nodes, nodes)
        return jnp.dot(dense_t[pl.ds(at, nodes), :], row_grads, preferred_element_type=F32)

    order = outer_peers[::-1] + [outer]
    counter_first = iter(range(6 * outer_count))

    def give(src, dst, recv, row_to):
        post(src, dst, first_send.at[next(counter_first)], recv, row_to, rep)

    def taken(dst, recv):
        remote(dst, dst, first_send.at[0], recv, plane_x, rep).wait_recv()

    def first_step(o):
        c = o * INNER + inner_d
        terms[c] = term_of(c).astype(BF16)
        give(terms.at[c, low], relay_in.at[0, o], relay_sem.at[0, o], plane_x)
        give(terms.at[c, high], relay_in.at[1, o], relay_sem.at[1, o], plane_y)
        for way, i, plane in ((0, inner_y, plane_y), (1, inner_x, plane_x)):
            c = o * INNER + i
            value = term_of(c)
            top, bottom = value[:nodes // 2], value[nodes // 2:]
            ready, kept = (bottom, top) if way == 0 else (top, bottom)
            at = high if way == 0 else low
            terms[c, at] = ready.astype(BF16)
            give(terms.at[c, at], first_in.at[way, o, at], first_recv.at[2 * way, o], plane)
            own_half[way, o] = kept
        own_terms[o] = term_of(o * INNER + inner)

    def second_step(o):
        for way, i, plane in ((0, inner_y, plane_y), (1, inner_x, plane_x)):
            c = o * INNER + i
            at = low if way == 0 else high
            taken(relay_in.at[way, o], relay_sem.at[way, o])
            terms[c, at] = (own_half[way, o] + relay_in[way, o].astype(F32)).astype(BF16)
            give(terms.at[c, at], first_in.at[way, o, at], first_recv.at[2 * way + 1, o], plane)

    def third_step(d, o):
        for way in range(2):
            for stage in range(2):
                at = low if (way == 0) == (stage == 1) else high
                taken(first_in.at[way, o, at], first_recv.at[2 * way + stage, o])
        total = own_terms[o] + first_in[0, o].astype(F32) + first_in[1, o].astype(F32)
        if d < outer_count - 1:
            second_out[d] = total.astype(BF16)
            post(
                second_out.at[d], second_in.at[outer], second_send.at[d],
                second_recv.at[outer], o * INNER + inner, rep,
            )
        return total

    def w_send_terms():
        column = pl.multiple_of((rep % 2) * half, half)
        w_full[...] = lax.dot_general(
            shared[0].reshape(n_rep * nodes, width), row_pre_grads,
            (((0,), (0,)), ((), ())), preferred_element_type=F32,
        )
        w_half = w_full[:, pl.ds(column, half)]
        for b in range(n_rows):
            w_out[b] = w_half[b * piece:(b + 1) * piece].astype(w_out.dtype)
        for n, to in enumerate(row_peers):
            post(w_out.at[to], w_in.at[row], w_send.at[n], w_recv.at[row], to, rep)
        w_in[row] = w_out[row]

    def w_send_sums():
        for to in row_peers:
            remote(w_out.at[to], w_in.at[to], w_send.at[0], w_recv.at[to], to, rep).wait_recv()
        side = rep % 2
        w_all[side, row] = jnp.sum(w_in[...].astype(F32), axis=0).astype(w_all.dtype)
        for n, to in enumerate(row_peers):
            post(w_all.at[side, row], w_all.at[side, row], wa_send.at[n], wa_recv.at[row], to, rep)

    def w_swap():
        side = rep % 2
        for to in row_peers:
            block = w_all.at[side, to]
            remote(block, block, wa_send.at[0], wa_recv.at[to], to, rep).wait_recv()
        post(w_all.at[side], w_all.at[side], swap_send, swap_recv, row, (rep + 1) % n_rep)

    def w_finish():
        other = w_all.at[(rep + 1) % 2]
        remote(other, other, swap_send, swap_recv, row, (rep + 1) % n_rep).wait_recv()
        whole = w_all[...].astype(F32)
        scale = lax.rsqrt(jnp.sum(whole * whole) / (width * width) + 1e-06)
        for side in range(2):
            for b in range(n_rows):
                wstep_ref[b * piece:(b + 1) * piece, side * half:(side + 1) * half] = whole[side, b] * scale

    row_peers = [(row + d) % n_rows for d in range(1, n_rows)]
    first_step(order[0])
    if outer_count > 1:
        first_step(order[1])
    w_send_terms()
    for d, o in enumerate(order):
        second_step(o)
        if d + 2 < outer_count:
            first_step(order[d + 2])
        if d > 0:
            third_step(d - 1, order[d - 1])
        if d == min(2, outer_count - 1):
            w_send_sums()
    total = third_step(outer_count - 1, outer)
    w_swap()
    w_finish()

    for o in outer_peers:
        remote(
            terms.at[0], second_in.at[o], second_send.at[0], second_recv.at[o],
            o * INNER + inner, rep,
        ).wait_recv()
        total = total + second_in[o].astype(F32)
    fgrad_ref[...] = total.astype(BF16)

    for copy in pending:
        copy.wait_send()


def body(n_rows, n_rep, features, weight, adj_tiles, tile_cols, tile_counts, out_grad, train_mask):
    nodes, width = features.shape
    tile_rows, tile = adj_tiles.shape[0], adj_tiles.shape[-1]
    outer_count = n_rows // INNER
    piece = width // n_rows
    half = width // 2
    w_type = BF16 if piece % 16 == 0 else F32
    vmem = pl.BlockSpec(memory_space=pltpu.VMEM)
    smem = pl.BlockSpec(memory_space=pltpu.SMEM)
    hbm = pl.BlockSpec(memory_space=pltpu.HBM)
    half_block = (nodes // 2, width)
    dma = pltpu.SemaphoreType.DMA
    vmem_bytes = int((53.8 if n_rows <= 16 else 63) * 1024 * 1024)
    block = (nodes, width)
    return pl.pallas_call(
        functools.partial(layer_kernel, n_rows, n_rep),
        out_shape=(
            jax.ShapeDtypeStruct(block, BF16),
            jax.ShapeDtypeStruct(block, BF16),
            jax.ShapeDtypeStruct((width, width), F32),
        ),
        in_specs=[hbm, hbm, hbm, smem, smem, hbm, hbm],
        out_specs=(vmem, vmem, vmem),
        scratch_shapes=[
            pltpu.VMEM(weight.shape, BF16),
            pltpu.VMEM(adj_tiles.shape, BF16),
            pltpu.VMEM(block, BF16),
            pltpu.VMEM((1, nodes), jnp.int32),
            pltpu.VMEM((n_rows,) + block, BF16),
            pltpu.VMEM((tile_rows * tile, n_rows * tile), BF16),
            pltpu.VMEM((n_rows * tile, tile_rows * tile), BF16),
            pltpu.VMEM((nodes, nodes), F32),
            pltpu.VMEM((n_rep,) + block, F32),
            pltpu.VMEM((n_rep,) + block, F32),
            pltpu.VMEM((2, n_rep) + block, BF16),
            pltpu.VMEM((width, width), F32),
            pltpu.VMEM((n_rows, piece, half), w_type),
            pltpu.VMEM((n_rows, piece, half), w_type),
            pltpu.VMEM((2, n_rows, piece, half), w_type),
            pltpu.VMEM((n_rows,) + block, BF16),
            pltpu.VMEM((2, outer_count) + half_block, F32),
            pltpu.VMEM((outer_count,) + block, F32),
            pltpu.VMEM((2, outer_count) + half_block, BF16),
            pltpu.VMEM((2, outer_count) + block, BF16),
            pltpu.VMEM((outer_count,) + block, BF16),
            pltpu.VMEM((outer_count,) + block, BF16),
            dma((5,)),
            dma((2 * n_rows,)), dma((n_rows,)), dma((n_rows,)),
            dma((n_rep,)), dma((n_rep,)),
            dma((2, n_rep)), dma((2, n_rep)),
            dma((n_rows,)), dma((n_rows,)),
            dma((n_rows,)), dma((n_rows,)),
            dma, dma,
            dma((6 * outer_count,)), dma((2, outer_count)), dma((4, outer_count)),
            dma((outer_count,)), dma((outer_count,)),
        ],
        compiler_params=pltpu.CompilerParams(
            collective_id=0, has_side_effects=True, vmem_limit_bytes=vmem_bytes
        ),
    )(
        features, weight, adj_tiles, tile_cols, tile_counts.reshape(-1),
        out_grad, train_mask.reshape(1, -1),
    )
def solution(mesh):
    placed = (
        P(("rows", "rep"), None),
        P(),
        P("rows", "rep", None, None, None),
        P("rows", "rep", None),
        P("rows", "rep"),
        P(("rows", "rep"), None),
        P(("rows", "rep")),
    )
    return jax.shard_map(
        functools.partial(body, mesh.shape["rows"], mesh.shape["rep"]),
        mesh=mesh,
        in_specs=placed,
        out_specs=(P(("rows", "rep"), None), P(("rows", "rep"), None), P()),
        check_vma=False,
    )
```
